256 devices in a mesh: row: 8 (over z), col: 32 (over x, y, core).
Axes of the slice: x: 4, y: 4, z: 8, core: 2. Of those that a mesh axis runs over, the one named last changes fastest.
Arguments:
- mask_field: float32 [3072, 12288], P('row', 'col'), may hold values from -1 to 1
- resist_goal: float32 [3072, 12288], P('row', 'col'), may hold values from 0 to 1
- kernels: float32 [8, 2, 64, 64], replicated, may hold values from -30 to 30
- colour: int32 [8, 32], P('row', 'col'), may hold values from 0 to 3
- active: int32 [8, 32], P('row', 'col'), may hold values 0 or 1
Outputs:
- final_mask: float32 [3072, 12288], P('row', 'col')
- next_tiles: float32 [4096, 16384], P('row', 'col')
The draws below stay inside these ranges and needn't reach their ends.
Inputs may be any that keep to these rules, and one draw needn't show every extreme that they name: Every entry of `colour` is 0, 1, 2 or 3, and neighbouring tiles may have the same colour.
All inputs are finite; a program needn't handle non-finite values. No bound on the sum of `active` on one device may be relied on, other than what follows from the above.
Results may differ from the reference program's by a relative error of at most 0.0035.
Values may be sent and summed in bfloat16 or wider, within the bound.
No kernel may reach another device: no remote copies, remote signals or barrier semaphores. Data moves between devices by JAX's collectives and lax.ppermute only.
A program may use at most 64 MiB of HBM per device.

```python
import math
import jax
import jax.numpy as jnp
from jax import lax

TILE = 512
HALO = 64
FREQS = 64
KERN = 8
ITERS = 2
CORE = 384
NR = 3072
NC = 12288
N_ROW = 8
N_COL = 32


def set_ends(array, own_key, low, top_value):
    longest = array.shape.index(max(array.shape))
    spots = []
    for shift in (0, 1):
        where = [jax.random.randint(jax.random.fold_in(own_key, axis), (), 0, length) for axis, length in enumerate(array.shape)]
        where[longest] = (where[longest] + shift) % array.shape[longest]
        spots.append(tuple(where))
    return array.at[spots[0]].set(low).at[spots[1]].set(top_value)


def levels(stream_key, shape, shards, least, largest):
    def one(axis_at, shards_of):
        steps = jax.random.uniform(jax.random.fold_in(jax.random.fold_in(stream_key, 6), axis_at), (shards_of,), jnp.float32, least / len(shards), largest / len(shards))
        return jnp.repeat(jnp.exp(steps), shape[axis_at] // shards_of).reshape((-1,) + (1,) * (len(shape) - axis_at - 1))

    level = one(*shards[0])
    for cut in shards[1:]:
        level = level * one(*cut)
    return level


def bell_draw(rng, extent, width, bound, held_as=jnp.bfloat16):
    values = jax.random.normal(rng, extent, jnp.float32) * width
    return jnp.minimum(jnp.maximum(values, -bound), bound).astype(held_as)


def setup_inputs(seed: int = 0) -> dict:
    streams_of = jax.random.split(jax.random.key(seed), 6)
    mask_field = jnp.clip(jax.random.uniform(streams_of[0], (NR, NC), jnp.float32, -1.0, 1.0) * levels(streams_of[0], (NR, NC), ((0, 8), (1, 32)), -0.4, 0.0), -1.0, 1.0)
    resist_goal = jnp.clip(1.0 * jax.random.uniform(streams_of[1], (NR, NC), jnp.float32) ** levels(streams_of[1], (NR, NC), ((0, 8), (1, 32)), -0.2, 0.2), 0.0, 1.0)
    kernels = bell_draw(streams_of[2], (KERN, 2, FREQS, FREQS), (0.625 * TILE / FREQS), 30.0, jnp.float32)
    colour = set_ends(jax.random.randint(streams_of[3], (N_ROW, N_COL), 0, 4), jax.random.fold_in(streams_of[3], 1), 0, 3).astype(jnp.int32)
    active = set_ends((jax.random.randint(streams_of[4], (N_ROW, N_COL), 0, 4) < 3).astype(jnp.int32), jax.random.fold_in(streams_of[4], 1), 0, 1)
    return dict(mask_field=mask_field, resist_goal=resist_goal, kernels=kernels, colour=colour, active=active)


STEP_SIZE = 0.05
STEEPNESS = 4.0
THRESHOLD = 1.0

def make_tables(tile_len, freq_count):
    position = jnp.arange(tile_len, dtype=jnp.int32)
    frequency = jnp.arange(freq_count, dtype=jnp.int32) - freq_count // 2
    phases = frequency[:, None] * position[None, :] % tile_len
    angles = phases.astype(jnp.float32) * (2.0 * math.pi / tile_len)
    cosine = jnp.cos(angles)
    sine_part = jnp.sin(angles)
    forward_table = (jnp.concatenate([cosine, sine_part], 0).T / tile_len).astype(jnp.bfloat16)
    inverse_table = jnp.concatenate([cosine, sine_part], 0).T.astype(jnp.bfloat16)
    return (forward_table, cosine / tile_len, sine_part / tile_len, cosine, sine_part, inverse_table)

def tile_loss(extended, goal_block, kernels, tables):
    forward_table, cos_fwd, sin_fwd, cos_inv, sin_inv, inverse_table = tables
    freq_count = cos_fwd.shape[0]
    tile_len = extended.shape[0]
    core_len = goal_block.shape[0]
    halo_width = (tile_len - core_len) // 2
    highest = lax.Precision.HIGHEST
    partial_value = jnp.dot(extended.astype(jnp.bfloat16), forward_table, preferred_element_type=jnp.float32)
    part_cos = partial_value[:, :freq_count]
    part_sin = partial_value[:, freq_count:]
    spec_real = jnp.dot(cos_fwd, part_cos, precision=highest) - jnp.dot(sin_fwd, part_sin, precision=highest)
    spec_imag = -(jnp.dot(cos_fwd, part_sin, precision=highest) + jnp.dot(sin_fwd, part_cos, precision=highest))
    kern_real = kernels[:, 0]
    kern_imag = kernels[:, 1]
    filt_real = kern_real * spec_real - kern_imag * spec_imag
    filt_imag = kern_real * spec_imag + kern_imag * spec_real
    half_real = jnp.einsum('kab,by->kay', filt_real, cos_inv, precision=highest) - jnp.einsum('kab,by->kay', filt_imag, sin_inv, precision=highest)
    half_imag = jnp.einsum('kab,by->kay', filt_real, sin_inv, precision=highest) + jnp.einsum('kab,by->kay', filt_imag, cos_inv, precision=highest)
    upper_half = jnp.stack([half_real, half_imag], 1)
    lower_half = jnp.stack([-half_imag, half_real], 1)
    stacked = jnp.concatenate([upper_half, lower_half], 2)
    stacked = jnp.transpose(stacked, (2, 0, 1, 3)).reshape(2 * freq_count, -1).astype(jnp.bfloat16)
    fields = jnp.dot(inverse_table, stacked, preferred_element_type=jnp.float32)
    fields = fields.reshape(tile_len, -1, tile_len)
    intensity = lax.optimization_barrier(jnp.sum(fields * fields, axis=1))
    resist = jax.nn.sigmoid(STEEPNESS * (intensity - THRESHOLD))
    inner_part = resist[halo_width:halo_width + core_len, halo_width:halo_width + core_len]
    differ = inner_part - goal_block
    return jnp.sum(differ * differ)

def tile_gradient(extended, goal_block, kernels, tables):
    loss_value, pullback = jax.vjp(lambda pixels: tile_loss(pixels, goal_block, kernels, tables), extended)
    return pullback(jnp.ones_like(loss_value))[0]

def reference(mask_field, resist_goal, kernels, colour, active):
    tables = make_tables(TILE, FREQS)
    update_tiles = (colour == 0).astype(jnp.float32)
    update_pixels = jnp.repeat(jnp.repeat(update_tiles, CORE, axis=0), CORE, axis=1)
    weights = active.astype(jnp.float32)
    current = mask_field
    for iteration in range(ITERS):
        padded = jnp.pad(current, HALO)

        def add_tile(tile_index, summed):
            row_at = (tile_index // N_COL).astype(jnp.int32)
            col_at = (tile_index % N_COL).astype(jnp.int32)
            top_row = (row_at * CORE).astype(jnp.int32)
            left_col = (col_at * CORE).astype(jnp.int32)
            extended = lax.dynamic_slice(padded, (top_row, left_col), (TILE, TILE))
            goal_block = lax.dynamic_slice(resist_goal, (top_row, left_col), (CORE, CORE))
            gradient = tile_gradient(extended, goal_block, kernels, tables) * weights[row_at, col_at]
            window = lax.dynamic_slice(summed, (top_row, left_col), (TILE, TILE))
            return lax.dynamic_update_slice(summed, window + gradient, (top_row, left_col))
        summed = lax.fori_loop(0, N_ROW * N_COL, add_tile, jnp.zeros_like(padded))
        gradient = summed[HALO:HALO + N_ROW * CORE, HALO:HALO + N_COL * CORE]
        current = jnp.clip(current - STEP_SIZE * update_pixels * gradient, -1.0, 1.0)
    padded = jnp.pad(current, HALO)

    def place_tile(tile_index, output):
        row_at = (tile_index // N_COL).astype(jnp.int32)
        col_at = (tile_index % N_COL).astype(jnp.int32)
        extended = lax.dynamic_slice(padded, ((row_at * CORE).astype(jnp.int32), (col_at * CORE).astype(jnp.int32)), (TILE, TILE))
        return lax.dynamic_update_slice(output, extended, ((row_at * TILE).astype(jnp.int32), (col_at * TILE).astype(jnp.int32)))
    next_tiles = lax.fori_loop(0, N_ROW * N_COL, place_tile, jnp.zeros((N_ROW * TILE, N_COL * TILE), jnp.float32))
    return (current, next_tiles)
```

```python
import math

import jax
import jax.numpy as jnp
import numpy as np
from jax import lax
from jax.experimental import pallas as pl
from jax.experimental.pallas import tpu as pltpu
from jax.sharding import PartitionSpec as P

TILE = 512
HALO = 64
FREQS = 64
KERN = 8
CORE = TILE - 2 * HALO
GRID = 128
LAP = 2 * HALO
FLAG = 16
SPEC = FREQS + FLAG
STEP_SIZE = 0.05
STEEPNESS = 4.0
THRESHOLD = 1.0
F32 = jnp.float32
BF16 = jnp.bfloat16


def waves(points, length):
    frequency = np.arange(FREQS) - FREQS // 2
    phases = (frequency[:, None] * np.asarray(points)[None, :]) % length
    angles = phases * (2.0 * math.pi / length)
    return np.cos(angles), np.sin(angles)


def halves(table):
    table = np.asarray(table, np.float32)
    high = table.astype(BF16)
    low = (table - high.astype(np.float32)).astype(BF16)
    return high, low


def constants():
    cosine, sine = waves(np.arange(TILE), TILE)
    coarse_cos, coarse_sin = waves(np.arange(GRID), GRID)
    stacked = np.concatenate([cosine, sine], 0)
    forward = (stacked.T / TILE).astype(np.float32).astype(BF16)
    left = halves(stacked / TILE)
    spread = halves(np.block([[coarse_cos, coarse_sin], [-coarse_sin, coarse_cos]]))
    column = halves(np.concatenate([coarse_cos, coarse_sin], 0).T)
    distance = np.arange(HALO, HALO + CORE)[:, None] - (TILE // GRID) * np.arange(GRID)[None, :]
    orders = np.arange(1, FREQS)
    angles = (orders * distance[:, :, None]) % TILE * (2.0 * math.pi / TILE)
    fill = halves((1.0 + 2.0 * np.cos(angles).sum(-1)) / GRID)
    rows = halves(stacked.T)
    sums = (np.concatenate([cosine, -sine], 0) / TILE).astype(np.float32).astype(BF16)
    return dict(
        forward=forward,
        left_h=left[0],
        left_l=left[1],
        spread_h=spread[0],
        spread_l=spread[1],
        gather_h=spread[0].T,
        column_h=column[0],
        column_t=column[0].T,
        fill_h=fill[0],
        fill_l=fill[1],
        fill_ht=fill[0].T,
        fill_lt=fill[1].T,
        rows_h=rows[0],
        sums=sums,
    )


IMAGE_TABLES = (
    "forward", "left_h", "left_l", "spread_h", "spread_l", "gather_h", "column_h", "column_t",
    "fill_h", "fill_l", "fill_ht", "fill_lt",
)
WAVE_TABLES = ("rows_h", "sums")


def dot(a, b):
    return jnp.dot(a, b, preferred_element_type=F32)


def split(value):
    high = value.astype(BF16)
    return high, (value - high.astype(F32)).astype(BF16)


def dot3(a, b):
    return dot(a[0], b[0]) + (dot(a[0], b[1]) + dot(a[1], b[0]))


def lane_sign(shape):
    lane = lax.broadcasted_iota(jnp.int32, shape, 1)
    return jnp.where(lane < FREQS, 1.0, -1.0).astype(F32)


def swapped(value):
    return pltpu.roll(value, FREQS, 1)


def image(window, goal, kern, active, flag, t, field_ref, spec_ref):
    sign = lane_sign((FREQS, 2 * FREQS))
    partial = dot(window.astype(BF16), t["forward"][...])
    mixed = dot3((t["left_h"][...], t["left_l"][...]), split(partial))
    spec = mixed[:FREQS] * sign - swapped(mixed[FREQS:])
    turned = -sign * swapped(spec)
    spread = (t["spread_h"][...], t["spread_l"][...])
    column = t["column_h"][...]
    total = jnp.zeros((GRID, 2 * GRID), F32)
    for k in range(KERN):
        real, imag = kern[k, 0], kern[k, 1]
        filtered = jnp.concatenate([real * spec + imag * turned, real * turned - imag * spec], 0)
        half = dot3(split(filtered), spread)
        field = dot(column, half.astype(BF16))
        field_ref[k] = field
        total = total + field * field
    coarse = total[:, :GRID] + total[:, GRID:]
    rowwise = dot3((t["fill_h"][...], t["fill_l"][...]), split(coarse))
    intensity = dot3(split(rowwise), (t["fill_ht"][...], t["fill_lt"][...]))
    resist = jax.nn.sigmoid(STEEPNESS * (intensity - THRESHOLD))
    slope = (4.0 * STEEPNESS) * (resist - goal) * (resist * (1.0 - resist))
    back = dot(t["fill_ht"][...], slope.astype(BF16))
    back = dot(back.astype(BF16), t["fill_h"][...])
    back = jnp.concatenate([back, back], 1)
    straight = jnp.zeros((FREQS, 2 * FREQS), F32)
    across = jnp.zeros((FREQS, 2 * FREQS), F32)
    for k in range(KERN):
        real, imag = kern[k, 0], kern[k, 1]
        cot = (back * field_ref[k]).astype(BF16)
        half = dot(t["column_t"][...], cot)
        pulled = dot(half.astype(BF16), t["gather_h"][...])
        upper, lower = pulled[:FREQS], pulled[FREQS:]
        straight = straight + (real * upper - imag * lower)
        across = across + (real * lower + imag * upper)
    result = (straight + sign * swapped(across)) * (active * (1.0 / TILE))
    spec_ref[:FREQS] = result.astype(BF16)
    spec_ref[FREQS:] = jnp.full((FLAG, 2 * FREQS), flag, F32).astype(BF16)


def choose(even, a, b):
    return jnp.where(even, a, b)


def first_kernel(*refs):
    n = len(IMAGE_TABLES)
    place, mask, goal, kern, near, far, side_near, side_far = refs[:8]
    tables = dict(zip(IMAGE_TABLES, refs[8 : 8 + n]))
    window, spec, field = refs[8 + n :]
    even_row, even_col = place[0] == 1, place[1] == 1
    up, down = place[2].astype(F32), place[3].astype(F32)
    left, right = place[4].astype(F32), place[5].astype(F32)
    above = choose(even_row, far[...], near[...]) * up
    below = choose(even_row, near[...], far[...]) * down
    before = choose(even_col, side_far[...], side_near[...]) * left
    after = choose(even_col, side_near[...], side_far[...]) * right
    window[HALO : HALO + CORE, HALO : HALO + CORE] = mask[...]
    window[:HALO, HALO : HALO + CORE] = above
    window[HALO + CORE :, HALO : HALO + CORE] = below
    half = TILE // 2
    window[:half, :HALO] = before[:, :HALO]
    window[half:, :HALO] = before[:, HALO:]
    window[:half, HALO + CORE :] = after[:, :HALO]
    window[half:, HALO + CORE :] = after[:, HALO:]
    image(window[...], goal[...], kern, place[6].astype(F32), place[7].astype(F32), tables, field, spec)


def pack_kernel(place, mask, near, far, side_one, side_two):
    even_row, even_col = place[0] == 1, place[1] == 1
    up, down = place[2].astype(F32), place[3].astype(F32)
    above = choose(even_row, far[...], near[...]) * up
    below = choose(even_row, near[...], far[...]) * down
    half = TILE // 2
    cut = half - HALO

    def strip(low):
        top = jnp.concatenate([above[:, low : low + HALO], mask[:cut, low : low + HALO]], 0)
        bottom = jnp.concatenate([mask[cut:, low : low + HALO], below[:, low : low + HALO]], 0)
        return jnp.concatenate([top, bottom], 1)

    first, last = strip(0), strip(CORE - HALO)
    side_one[...] = choose(even_col, last, first)
    side_two[...] = choose(even_col, first, last)


def updated(place, window, packed, side_near, side_far, t):
    even_row, even_col = place[0] == 1, place[1] == 1
    up, down = place[2].astype(F32), place[3].astype(F32)
    left, right = place[4].astype(F32), place[5].astype(F32)
    sign = lane_sign((FREQS, 2 * FREQS))
    lane = lax.broadcasted_iota(jnp.int32, (1, 2 * FREQS), 1)

    def parts(triple, scale):
        own, one, two = (triple[i * SPEC : (i + 1) * SPEC].astype(F32) for i in range(3))
        above = choose(even_row, two, one) * (up * scale)
        below = choose(even_row, one, two) * (down * scale)
        return above, own * scale, below

    near, far = side_near[...], side_far[...]
    columns = (
        parts(choose(even_col, far, near), left),
        parts(packed[...], 1.0),
        parts(choose(even_col, near, far), right),
    )

    def square(value):
        value = value[:FREQS]
        return jnp.concatenate([value, -sign * swapped(value)], 0).astype(BF16)

    above, own, below = (
        jnp.concatenate([square(columns[j][i]) for j in range(3)], 1) for i in range(3)
    )
    rows = t["rows_h"][...]
    top, middle, bottom = rows[:LAP], rows[LAP:CORE], rows[CORE:]
    sums = jnp.concatenate(
        [
            dot(top, own) + dot(bottom, above),
            dot(middle, own),
            dot(bottom, own) + dot(top, below),
        ],
        0,
    ).astype(BF16)
    wide = 2 * FREQS
    q_left, q_own, q_right = sums[:, :wide], sums[:, wide : 2 * wide], sums[:, 2 * wide :]
    table = t["sums"][...]
    first, centre, last = table[:, :LAP], table[:, LAP:CORE], table[:, CORE:]
    gradient = jnp.concatenate(
        [
            dot(q_own, first) + dot(q_left, last),
            dot(q_own, centre),
            dot(q_own, last) + dot(q_right, first),
        ],
        1,
    )

    def scale(i):
        flags = [columns[j][i][FREQS : FREQS + 1] for j in range(3)]
        return STEP_SIZE * jnp.concatenate(
            [
                jnp.where(lane < HALO, flags[0], flags[1]),
                flags[1],
                flags[1],
                jnp.where(lane < HALO, flags[1], flags[2]),
            ],
            1,
        )

    moved = jnp.concatenate(
        [
            gradient[:HALO] * scale(0),
            gradient[HALO : HALO + CORE] * scale(1),
            gradient[HALO + CORE :] * scale(2),
        ],
        0,
    )
    return jnp.clip(window[...] - moved, -1.0, 1.0)


def middle_kernel(*refs):
    n, m = len(IMAGE_TABLES), len(WAVE_TABLES)
    place, before, goal, kern, packed, side_near, side_far = refs[:7]
    tables = dict(zip(IMAGE_TABLES + WAVE_TABLES, refs[7 : 7 + n + m]))
    window, spec, field = refs[7 + n + m :]
    window[...] = updated(place, before, packed, side_near, side_far, tables)
    image(window[...], goal[...], kern, place[6].astype(F32), place[7].astype(F32), tables, field, spec)


def last_kernel(place, before, packed, side_near, side_far, rows_h, sums, mask, window):
    tables = dict(rows_h=rows_h, sums=sums)
    window[...] = updated(place, before, packed, side_near, side_far, tables)
    mask[...] = window[HALO : HALO + CORE, HALO : HALO + CORE]


def call(kernel, shapes, operands, scratch=(), name=None):
    vmem = pl.BlockSpec(memory_space=pltpu.VMEM)
    smem = pl.BlockSpec(memory_space=pltpu.SMEM)
    return pl.pallas_call(
        kernel,
        out_shape=shapes,
        in_specs=[smem] + [vmem] * (len(operands) - 1),
        out_specs=[vmem] * len(shapes),
        scratch_shapes=list(scratch),
        name=name,
    )(*operands)


def routes(axis):
    devices = lax.axis_size(axis)
    near = [(i, i ^ 1) for i in range(devices)]
    far = [(i, (((i + 1) ^ 1) - 1) % devices) for i in range(devices)]
    return near, far


def traded(one, two, axis):
    near, far = routes(axis)
    return lax.ppermute(one, axis, near), lax.ppermute(two, axis, far)


def traded_spectra(spec):
    near, far = traded(spec, spec, "row")
    packed = jnp.concatenate([spec, near, far], 0)
    side_near, side_far = traded(packed, packed, "col")
    return packed, side_near, side_far


def body(mask_field, resist_goal, kernels, colour, active):
    row, col = lax.axis_index("row"), lax.axis_index("col")
    rows, cols = lax.axis_size("row"), lax.axis_size("col")
    even_row, even_col = row % 2 == 0, col % 2 == 0
    place = jnp.stack(
        [
            x.astype(jnp.int32)
            for x in (
                even_row, even_col, row > 0, row < rows - 1, col > 0, col < cols - 1,
                active[0, 0], colour[0, 0] == 0,
            )
        ]
    )
    made = constants()
    tables = {name: jnp.asarray(value) for name, value in made.items()}
    image_tables = [tables[name] for name in IMAGE_TABLES]
    wave_tables = [tables[name] for name in WAVE_TABLES]
    kern = jnp.concatenate([kernels, kernels], -1)
    top, bottom = mask_field[:HALO], mask_field[CORE - HALO :]
    near, far = traded(
        jnp.where(even_row, bottom, top), jnp.where(even_row, top, bottom), "row"
    )
    side = jax.ShapeDtypeStruct((TILE // 2, 2 * HALO), F32)
    one, two = call(pack_kernel, [side, side], [place, mask_field, near, far], name="pack")
    side_near, side_far = traded(one, two, "col")
    window_shape = jax.ShapeDtypeStruct((TILE, TILE), F32)
    mask_shape = jax.ShapeDtypeStruct((CORE, CORE), F32)
    spec_shape = jax.ShapeDtypeStruct((SPEC, 2 * FREQS), BF16)
    field = pltpu.VMEM((KERN, GRID, 2 * GRID), F32)
    window, spec = call(
        first_kernel,
        [window_shape, spec_shape],
        [place, mask_field, resist_goal, kern, near, far, side_near, side_far] + image_tables,
        [field],
        name="first",
    )
    window, spec = call(
        middle_kernel,
        [window_shape, spec_shape],
        [place, window, resist_goal, kern, *traded_spectra(spec)] + image_tables + wave_tables,
        [field],
        name="middle",
    )
    final_mask, final_tile = call(
        last_kernel,
        [mask_shape, window_shape],
        [place, window, *traded_spectra(spec)] + wave_tables,
        name="last",
    )
    return final_mask, final_tile


def solution(mesh):
    return jax.shard_map(
        body,
        mesh=mesh,
        in_specs=(P("row", "col"), P("row", "col"), P(), P("row", "col"), P("row", "col")),
        out_specs=(P("row", "col"), P("row", "col")),
        check_vma=False,
    )
```

```python
import math

import jax
import jax.numpy as jnp
import numpy as np
from jax import lax
from jax.experimental import pallas as pl
from jax.experimental.pallas import tpu as pltpu
from jax.sharding import PartitionSpec as P

TILE = 512
HALO = 64
FREQS = 64
KERN = 8
CORE = TILE - 2 * HALO
GRID = 128
LAP = 2 * HALO
DC = FREQS // 2
GRANT = 16 << 20
WIDE = 2 * FREQS
STEP_SIZE = 0.05
STEEPNESS = 4.0
THRESHOLD = 1.0
F32 = jnp.float32
BF16 = jnp.bfloat16


def waves(points, length):
    frequency = np.arange(FREQS) - FREQS // 2
    phases = (frequency[:, None] * np.asarray(points)[None, :]) % length
    angles = phases * (2.0 * math.pi / length)
    return np.cos(angles), np.sin(angles)


def rounded(table):
    return np.asarray(table, np.float32).astype(BF16)


def constants():
    cosine, sine = waves(np.arange(TILE), TILE)
    coarse_cos, coarse_sin = waves(np.arange(GRID), GRID)
    stacked = np.concatenate([cosine, sine], 0)
    forward = rounded(stacked.T / TILE)
    left = rounded(stacked / TILE)
    spread = rounded(np.block([[coarse_cos, coarse_sin], [-coarse_sin, coarse_cos]]))
    column = rounded(np.concatenate([coarse_cos, coarse_sin], 0).T)
    distance = np.arange(HALO, HALO + CORE)[:, None] - (TILE // GRID) * np.arange(GRID)[None, :]
    orders = np.arange(1, FREQS)
    angles = (orders * distance[:, :, None]) % TILE * (2.0 * math.pi / TILE)
    fill = rounded((1.0 + 2.0 * np.cos(angles).sum(-1)) / GRID)
    return dict(
        forward_core=forward[HALO : HALO + CORE],
        forward_side=np.concatenate([forward[:HALO], forward[HALO + CORE :]], 0),
        forward_inner=forward[LAP:CORE],
        forward_edge=np.concatenate([forward[:LAP], forward[CORE:]], 0),
        left=left,
        left_halves=np.concatenate([left[:, : TILE // 2], left[:, TILE // 2 :]], 0),
        spread=spread,
        gather=spread.T,
        column=column,
        column_t=column.T,
        fill=fill,
        fill_t=fill.T,
        rows_outer=rounded(
            np.block(
                [
                    [cosine.T[:LAP], cosine.T[CORE:]],
                    [sine.T[:LAP], sine.T[CORE:]],
                    [cosine.T[CORE:], cosine.T[:LAP]],
                    [sine.T[CORE:], sine.T[:LAP]],
                ]
            )
        ),
        rows_inner=rounded(np.concatenate([cosine.T[LAP:CORE], sine.T[LAP:CORE]], 0)),
        sums=rounded(np.concatenate([cosine, -sine, -sine, -cosine], 0) / TILE),
    )


IMAGE_TABLES = ("spread", "gather", "column", "column_t", "fill", "fill_t")
WAVE_TABLES = ("rows_outer", "rows_inner", "sums")


def dot(a, b):
    return jnp.dot(a, b, preferred_element_type=F32)


def lanes(shape):
    return lax.broadcasted_iota(jnp.int32, shape, len(shape) - 1)


def swapped(value):
    return pltpu.roll(value, FREQS, 1)


def choose(even, a, b):
    return jnp.where(even, a, b)


def where_am_i():
    row, col = lax.axis_index("row"), lax.axis_index("col")
    rows, cols = lax.axis_size("row"), lax.axis_size("col")
    even = (row & 1) == 0, (col & 1) == 0
    inside = (row > 0, row < rows - 1, col > 0, col < cols - 1)
    return (*even, *(x.astype(F32) for x in inside))


def ordered(even, near, far, low, high):
    low, high = low.astype(near.dtype), high.astype(near.dtype)
    return choose(even, far, near) * low, choose(even, near, far) * high


def image(mixed, goal, kern, flags, t, field_ref, spec_ref):
    sign = jnp.where(lanes((FREQS, WIDE)) < FREQS, 1.0, -1.0).astype(F32)
    spec = mixed[:FREQS] * sign - swapped(mixed[FREQS:])
    turned = -sign * swapped(spec)
    filtered = jnp.concatenate(
        [kern[k, 0] * spec + kern[k, 1] * turned for k in range(KERN)], 0
    )
    half = dot(filtered.astype(BF16), t["spread"][...]).astype(BF16)
    column = t["column"][...]
    total = jnp.zeros((GRID, 2 * GRID), F32)
    for k in range(KERN):
        part = half[k * FREQS : (k + 1) * FREQS]
        cross = jnp.concatenate([-part[:, GRID:], part[:, :GRID]], 1)
        field = dot(column, jnp.concatenate([part, cross], 0))
        field_ref[k] = field.astype(BF16)
        total = total + field * field
    coarse = total[:, :GRID] + total[:, GRID:]
    rowwise = dot(t["fill"][...], coarse.astype(BF16))
    intensity = dot(rowwise.astype(BF16), t["fill_t"][...])
    resist = jax.nn.sigmoid(STEEPNESS * (intensity - THRESHOLD))
    slope = (4.0 * STEEPNESS) * (resist - goal) * (resist * (1.0 - resist))
    back = dot(t["fill_t"][...], slope.astype(BF16))
    back = dot(back.astype(BF16), t["fill"][...])
    back = jnp.concatenate([back, back], 1).astype(BF16)
    gathered = jnp.concatenate(
        [dot(back * field_ref[k], t["gather"][...]).astype(BF16) for k in range(KERN)], 0
    )
    column_t = t["column_t"][...]
    straight = jnp.zeros((FREQS, WIDE), F32)
    across = jnp.zeros((FREQS, WIDE), F32)
    for k in range(KERN):
        real, imag = kern[k, 0], kern[k, 1]
        part = dot(column_t, gathered[k * GRID : (k + 1) * GRID])
        upper, lower = part[:FREQS], part[FREQS:]
        straight = straight + (real * upper - imag * lower)
        across = across + (real * lower + imag * upper)
    result = (straight + sign * swapped(across)) * (flags[0:1, 0:1].astype(F32) * (1.0 / TILE))
    row = lax.broadcasted_iota(jnp.int32, (FREQS, WIDE), 0)
    spare = (row == DC) & (lanes((FREQS, WIDE)) == FREQS + DC)
    owned = (flags[8:9, 0:1] == 0).astype(F32)
    spec_ref[...] = jnp.where(spare, owned, result).astype(BF16)


def prep_kernel(after, raw, kern):
    del after
    for k in range(KERN):
        for part in range(2):
            value = raw[k, part]
            kern[k, part] = jnp.concatenate([value, value], 1)


def strips_kernel(mask, near, far, held, sems):
    even_row = where_am_i()[0]
    cuts = ((0, HALO), (CORE - HALO, HALO), (HALO, CORE - 2 * HALO))
    copies = [
        pltpu.make_async_copy(mask.at[pl.ds(*cut)], held.at[pl.ds(*cut)], sems.at[i])
        for i, cut in enumerate(cuts)
    ]
    for copy in copies:
        copy.start()
    copies[0].wait()
    copies[1].wait()
    first, last = held[:HALO].astype(BF16), held[CORE - HALO :].astype(BF16)
    near[...] = choose(even_row, last, first)
    far[...] = choose(even_row, first, last)
    copies[2].wait()


def pack_kernel(mask, near, far, side_one, side_two):
    even_row, even_col, up, down, _, _ = where_am_i()
    above, below = ordered(even_row, near[...], far[...], up, down)
    half = TILE // 2
    cut = half - HALO

    def strip(low):
        own = mask[:, low : low + HALO].astype(BF16)
        top = jnp.concatenate([above[:, low : low + HALO], own[:cut]], 0)
        bottom = jnp.concatenate([own[cut:], below[:, low : low + HALO]], 0)
        return jnp.concatenate([top, bottom], 1)

    first, last = strip(0), strip(CORE - HALO)
    side_one[...] = choose(even_col, last, first)
    side_two[...] = choose(even_col, first, last)


def core_kernel(mask, near, far, table, left, mixed):
    even_row, _, up, down, _, _ = where_am_i()
    above, below = ordered(even_row, near[...], far[...], up, down)
    held = jnp.concatenate([above, mask[...].astype(BF16), below], 0)
    mixed[...] = dot(left[...], dot(held, table[...]).astype(BF16))


def first_kernel(*refs):
    mixed, side_near, side_far, goal, kern, flags, halved, side_table = refs[:8]
    tables = dict(zip(IMAGE_TABLES, refs[8:]))
    spec, field = refs[-2:]
    _, even_col, _, _, left, right = where_am_i()
    before, after = ordered(even_col, side_near[...], side_far[...], left, right)
    wide = dot(halved[...], jnp.concatenate([before, after], 1))
    upper, lower = wide[:WIDE], wide[WIDE:]
    strips = jnp.where(
        lanes((WIDE, WIDE)) < HALO,
        upper[:, :WIDE] + swapped(lower[:, :WIDE]),
        swapped(upper[:, WIDE:]) + lower[:, WIDE:],
    )
    total = mixed[...] + dot(strips.astype(BF16), side_table[...])
    image(total, goal[...], kern, flags, tables, field, spec)


def triple(packed, even_row, up, down, scale):
    own, near, far = (packed[i * FREQS : (i + 1) * FREQS] for i in range(3))
    above, below = ordered(even_row, near, far, up * scale, down * scale)
    return above, own * scale.astype(BF16), below


def owned_step(spec):
    return STEP_SIZE * spec[DC : DC + 1, FREQS + DC : FREQS + DC + 1].astype(F32)


def along_rows(outer, inner, above, own, below):
    top = dot(outer[: 2 * LAP], jnp.concatenate([own, above], 0)).astype(BF16)
    middle = dot(inner[...], own).astype(BF16)
    end = dot(outer[2 * LAP :], jnp.concatenate([own, below], 0)).astype(BF16)
    results = []
    for low in range(0, own.shape[1], WIDE):
        parts = []
        for value in (top, middle, end):
            value, count = value[:, low : low + WIDE], value.shape[0] // 2
            parts.append(jnp.concatenate([value[:count], value[count:]], 1))
        results.append(jnp.concatenate(parts, 0))
    return results


def by_rows(values):
    counts = (HALO, CORE, HALO)
    return jnp.concatenate(
        [jnp.broadcast_to(v, (n, v.shape[1])) for v, n in zip(values, counts)], 0
    )


def own_gradient(own, near, far, rows_outer, rows_inner, sums):
    even_row, _, up, down, _, _ = where_am_i()
    packed = jnp.concatenate([own[...], near[...], far[...]], 0)
    parts = triple(packed, even_row, up, down, jnp.float32(1.0))
    (waves_here,) = along_rows(rows_outer, rows_inner, *parts)
    step = by_rows([jnp.broadcast_to(owned_step(x), (1, WIDE)) for x in parts])
    return dot(waves_here, sums[...]), step


def moved(old, gradient, step):
    return jnp.clip(old - step * gradient, -1.0, 1.0)


def outer_columns(gradient):
    return jnp.concatenate([gradient[:, :LAP], gradient[:, CORE:]], 1)


def assembled(mask, near, far, side_near, side_far):
    even_row, even_col, up, down, left, right = where_am_i()
    near, far, side_near, side_far = (x[...].astype(F32) for x in (near, far, side_near, side_far))
    above, below = ordered(even_row, near, far, up, down)
    before, after = ordered(even_col, side_near, side_far, left, right)
    tall = jnp.concatenate([above, mask[...], below], 0)
    turned = [pltpu.roll(tall[:, i * LAP : (i + 1) * LAP], HALO, 1) for i in range(3)]
    low = lanes((TILE, LAP)) < HALO
    before = jnp.concatenate([before, pltpu.roll(before, HALO, 1)], 0)
    after = jnp.concatenate([pltpu.roll(after, HALO, 1), after], 0)
    edges = jnp.concatenate(
        [jnp.where(low, before, turned[0]), jnp.where(low, turned[2], after)], 1
    )
    inner = jnp.concatenate(
        [jnp.where(low, turned[0], turned[1]), jnp.where(low, turned[1], turned[2])], 1
    )
    return edges, inner


def inner_kernel(
    mask, near, far, side_near, side_far, own, row_near, row_far, rows_outer, rows_inner, sums, table,
    left, edges, outer, inner, mixed,
):
    gradient, step = own_gradient(own, row_near, row_far, rows_outer, rows_inner, sums)
    edges_now, inner_now = assembled(mask, near, far, side_near, side_far)
    edges[...] = edges_now
    outer[...] = outer_columns(gradient)
    result = moved(inner_now, gradient[:, LAP:CORE], jnp.concatenate([step, step], 1))
    inner[...] = result
    mixed[...] = dot(left[...], dot(result.astype(BF16), table[...]).astype(BF16))


def new_edges(edges, outer, packed, side_near, side_far, rows_outer, rows_inner, sums):
    even_row, even_col, up, down, left, right = where_am_i()
    near, far = side_near[...], side_far[...]
    west = triple(choose(even_col, far, near), even_row, up, down, left)
    here = triple(packed[...], even_row, up, down, jnp.float32(1.0))
    east = triple(choose(even_col, near, far), even_row, up, down, right)
    both = (jnp.concatenate([a, b], 1) for a, b in zip(west, east))
    first, second = along_rows(rows_outer, rows_inner, *both)
    added = jnp.concatenate([dot(first, sums[:, CORE:]), dot(second, sums[:, :LAP])], 1)
    low = lanes((1, WIDE)) < HALO
    steps = []
    for a, b, c in zip(west, here, east):
        a, b, c = (owned_step(x) for x in (a, b, c))
        steps.append(jnp.concatenate([jnp.where(low, a, b), jnp.where(low, b, c)], 1))
    return moved(edges[...], outer[...] + added, by_rows(steps))


def middle_kernel(*refs):
    edges, outer, mixed, packed, side_near, side_far, goal, kern, flags = refs[:9]
    rows_outer, rows_inner, sums, edge_table, left = refs[9:14]
    tables = dict(zip(IMAGE_TABLES, refs[14:]))
    edges_out, spec, field = refs[-3:]
    result = new_edges(edges, outer, packed, side_near, side_far, rows_outer, rows_inner, sums)
    edges_out[...] = result
    wide = dot(left[...], result.astype(BF16))
    total = mixed[...] + dot(wide.astype(BF16), edge_table[...])
    image(total, goal[...], kern, flags, tables, field, spec)


def close_kernel(inner, own, near, far, rows_outer, rows_inner, sums, outer, result, mask, tile, centre, sems):
    gradient, step = own_gradient(own, near, far, rows_outer, rows_inner, sums)
    outer[...] = outer_columns(gradient)
    now = moved(inner[...], gradient[:, LAP:CORE], jnp.concatenate([step, step], 1))
    result[...] = now
    whole = pltpu.make_async_copy(result, tile.at[:, LAP:CORE], sems.at[0])
    whole.start()
    now = now[HALO : HALO + CORE]
    low = lanes((CORE, LAP)) < HALO
    centre[...] = jnp.where(
        low, pltpu.roll(now[:, :LAP], HALO, 1), pltpu.roll(now[:, LAP:], HALO, 1)
    )
    part = pltpu.make_async_copy(centre, mask.at[:, LAP : 2 * LAP], sems.at[1])
    part.start()
    whole.wait()
    part.wait()


def last_kernel(
    edges, outer, packed, side_near, side_far, inner, rows_outer, rows_inner, sums, mask_in, tile_in,
    mask, tile, result, west, east, sems,
):
    del mask_in, tile_in
    now = new_edges(edges, outer, packed, side_near, side_far, rows_outer, rows_inner, sums)
    result[...] = now
    copies = [
        pltpu.make_async_copy(result.at[:, :LAP], tile.at[:, :LAP], sems.at[0]),
        pltpu.make_async_copy(result.at[:, LAP:], tile.at[:, CORE:], sems.at[1]),
        pltpu.make_async_copy(west, mask.at[:, :LAP], sems.at[2]),
        pltpu.make_async_copy(east, mask.at[:, 2 * LAP :], sems.at[3]),
    ]
    copies[0].start()
    copies[1].start()
    now = now[HALO : HALO + CORE]
    held = inner[HALO : HALO + CORE, :]
    low = lanes((CORE, LAP)) < HALO

    def joined(a, b):
        return jnp.where(low, pltpu.roll(a, HALO, 1), pltpu.roll(b, HALO, 1))

    west[...] = joined(now[:, :LAP], held[:, :LAP])
    copies[2].start()
    east[...] = joined(held[:, LAP:], now[:, LAP:])
    copies[3].start()
    for copy in copies:
        copy.wait()


VMEM = pl.BlockSpec(memory_space=pltpu.VMEM)
ANY = pl.BlockSpec(memory_space=pl.ANY)


def call(kernel, operands, shapes, scratch=(), held=(), far=(), name=None, aliases=None):
    placed = [pltpu.with_memory_space_constraint(x, pltpu.VMEM) for x in operands]
    return pl.pallas_call(
        kernel,
        out_shape=[pltpu.VMEM(s, d) for s, d in shapes]
        + [jax.ShapeDtypeStruct(s, F32) for s in far],
        in_specs=[VMEM] * len(operands) + [ANY] * len(held),
        out_specs=[VMEM] * len(shapes) + [ANY] * len(far),
        scratch_shapes=list(scratch),
        input_output_aliases=aliases or {},
        compiler_params=pltpu.CompilerParams(
            vmem_limit_bytes=GRANT
        ),
        name=name,
    )(*placed, *(pltpu.with_memory_space_constraint(x, pltpu.HBM) for x in held))


def routes(axis):
    devices = lax.axis_size(axis)
    near = [(i, i ^ 1) for i in range(devices)]
    far = [(i, (((i + 1) ^ 1) - 1) % devices) for i in range(devices)]
    return near, far


def traded(one, two, axis):
    near, far = routes(axis)
    return lax.ppermute(one, axis, near), lax.ppermute(two, axis, far)


def traded_spectra(spec):
    near, far = traded(spec, spec, "row")
    packed = jnp.concatenate([spec, near, far], 0)
    return (near, far), (packed, *traded(packed, packed, "col"))


def body(mask_field, resist_goal, kernels, colour, active):
    tables = {name: jnp.asarray(value) for name, value in constants().items()}
    image_tables = [tables[name] for name in IMAGE_TABLES]
    wave_tables = [tables[name] for name in WAVE_TABLES]
    strip = ((HALO, CORE), BF16)
    one, two, mask = call(
        strips_kernel,
        [],
        [strip, strip, ((CORE, CORE), F32)],
        [pltpu.SemaphoreType.DMA((3,))],
        held=[mask_field],
        name="strips",
    )
    near, far = traded(one, two, "row")
    core, tile = (CORE, CORE), (TILE, TILE)
    doubled = (KERN, 2, FREQS, WIDE)
    side = ((TILE // 2, 2 * HALO), BF16)
    one, two = call(pack_kernel, [mask, near, far], [side, side], name="pack")
    sides = traded(one, two, "col")
    (kern,) = call(prep_kernel, [one, kernels], [(doubled, F32)], name="prep")
    _, active, colour = lax.optimization_barrier((one, active, colour))
    spare = ((0, 7, 0), (0, WIDE - 1, 0))
    zero = jnp.int32(0)
    flags = jnp.concatenate([lax.pad(active, zero, spare), lax.pad(colour, zero, spare)], 0)
    mixed_shape, spec_shape = ((WIDE, WIDE), F32), ((FREQS, WIDE), BF16)
    pair_shape = ((TILE, 2 * LAP), F32)
    (mixed,) = call(
        core_kernel,
        [mask, near, far, tables["forward_core"], tables["left"]],
        [mixed_shape],
        name="core",
    )
    field = pltpu.VMEM((KERN, GRID, 2 * GRID), BF16)
    (spec,) = call(
        first_kernel,
        [mixed, *sides, resist_goal, kern, flags, tables["left_halves"], tables["forward_side"]]
        + image_tables,
        [spec_shape],
        [field],
        name="first",
    )
    rows, columns = traded_spectra(spec)
    edges, outer, inner, mixed = call(
        inner_kernel,
        [mask, near, far, *sides, spec, *rows]
        + wave_tables
        + [tables["forward_inner"], tables["left"]],
        [pair_shape, pair_shape, pair_shape, mixed_shape],
        name="inner",
    )
    edges, spec = call(
        middle_kernel,
        [edges, outer, mixed, *columns, resist_goal, kern, flags]
        + wave_tables
        + [tables["forward_edge"], tables["left"]]
        + image_tables,
        [pair_shape, spec_shape],
        [field],
        name="middle",
    )
    rows, columns = traded_spectra(spec)
    outer, inner, final_mask, final_tile = call(
        close_kernel,
        [inner, spec, *rows] + wave_tables,
        [pair_shape, pair_shape],
        [pltpu.VMEM((CORE, LAP), F32), pltpu.SemaphoreType.DMA((2,))],
        far=[core, tile],
        name="close",
    )
    return call(
        last_kernel,
        [edges, outer, *columns, inner] + wave_tables,
        [],
        [
            pltpu.VMEM((TILE, 2 * LAP), F32),
            pltpu.VMEM((CORE, LAP), F32),
            pltpu.VMEM((CORE, LAP), F32),
            pltpu.SemaphoreType.DMA((4,)),
        ],
        held=[final_mask, final_tile],
        far=[core, tile],
        name="last",
        aliases={9: 0, 10: 1},
    )


def solution(mesh):
    return jax.shard_map(
        body,
        mesh=mesh,
        in_specs=(P("row", "col"), P("row", "col"), P(), P("row", "col"), P("row", "col")),
        out_specs=(P("row", "col"), P("row", "col")),
        check_vma=False,
    )
```
